128 devices in a mesh: row: 8 (over x_hi, y), col: 16 (over z, x_lo, core).
Axes of the slice: x: 4 (x_hi: 2, x_lo: 2; x = x_hi * 2 + x_lo), y: 4, z: 4, core: 2. Of those that a mesh axis runs over, the one named last changes fastest.
Arguments:
- lower_left: float32 [12288, 16384], P('row', 'col'), may hold values from -0.0546875 to 0.0546875
- lower_cotan: float32 [12288, 16384], P('row', 'col'), may hold values from -6 to 6
- panel: float32 [12288, 512], P('row', 'col'), may hold values from -0.0546875 to 0.0546875
- panel_cotan: float32 [12288, 512], P('row', 'col'), may hold values from -6 to 6
- diag_factor: float32 [512, 512], P('row', 'col'), as said below
- inverse_factor: float32 [512, 512], P('row', 'col'), as said below
- diag_cotan: float32 [512, 512], P('row', 'col'), may hold values from -6 to 6
- row_factor: float32 [512, 16384], P('row', 'col'), may hold values from -0.25 to 0.25
- row_cotan: float32 [512, 16384], P('row', 'col'), may hold values from -6 to 6
Outputs:
- lower_grad: float32 [12288, 16384], P('row', 'col')
- panel_grad: float32 [12288, 512], P('row', 'col')
- diag_grad: float32 [512, 512], P('row', 'col')
- row_grad: float32 [512, 16384], P('row', 'col')
The draws below stay inside these ranges and needn't reach their ends.
Inputs may be any that keep to these rules, and one draw needn't show every extreme that they name: diag_factor is lower triangular with a positive diagonal, and inverse_factor is its inverse. inverse_factor is the inverse of diag_factor, lower triangular.
All inputs are finite; a program needn't handle non-finite values.
Results may differ from the reference program's by a relative error of at most 0.00016.
Values sent between devices are 32-bit elements; how exact they have to be, the bound alone decides.
No kernel may reach another device: no remote copies, remote signals or barrier semaphores. Data moves between devices by JAX's collectives and lax.ppermute only.
A program may use at most 128 MiB of HBM per device.

```python
import math
import jax
import jax.numpy as jnp
from jax import lax

NB = 512
M = 12288
K = 16384


def factor_pair(key):
    first = jax.random.fold_in(key, 11)
    second = jax.random.fold_in(key, 12)
    diagonal = jnp.exp(jax.random.uniform(first, (NB,), jnp.float32, 0.0, math.log(2.0)))
    spread = jnp.clip(jax.random.normal(second, (NB, NB), jnp.float32), -4.0, 4.0) * (0.6 / math.sqrt(NB))
    factor = jnp.tril(spread, -1) + jnp.diag(diagonal)
    inverse = jax.scipy.linalg.solve_triangular(factor, jnp.eye(NB, dtype=jnp.float32), lower=True)
    return (factor, jnp.tril(inverse))


def draw_diag_factor(key, part):
    return factor_pair(key)[0]


def draw_inverse_factor(key, part):
    return factor_pair(key)[1]


def block_scale(rng, extent, split, least, largest):
    def one(position, blocks):
        draws = jax.random.uniform(jax.random.fold_in(jax.random.fold_in(rng, 6), position), (blocks,), jnp.float32, least / len(split), largest / len(split))
        return jnp.repeat(jnp.exp(draws), extent[position] // blocks).reshape((-1,) + (1,) * (len(extent) - position - 1))

    factor_of = one(*split[0])
    for cut in split[1:]:
        factor_of = factor_of * one(*cut)
    return factor_of


def scatter_about(stream_key, shape, deviation, bound, cuts=(), kind=jnp.bfloat16):
    entries = deviation * jax.random.normal(stream_key, shape, jnp.float32)
    if cuts:
        entries = entries * block_scale(stream_key, shape, cuts, -0.22, 0.18)
    return jnp.clip(entries, -bound, bound).astype(kind)


def setup_inputs(seed: int = 0) -> dict:
    key_of = jax.random.split(jax.random.key(seed), 10)
    lower_left = scatter_about(key_of[0], (M, K), M ** -0.5, 0.0546875, ((0, 8), (1, 16)), jnp.float32)
    lower_cotan = scatter_about(key_of[1], (M, K), 1.0, 6.0, ((0, 8), (1, 16)), jnp.float32)
    panel = scatter_about(key_of[2], (M, NB), M ** -0.5, 0.0546875, ((0, 8), (1, 16)), jnp.float32)
    panel_cotan = scatter_about(key_of[3], (M, NB), 1.0, 6.0, ((0, 8), (1, 16)), jnp.float32)
    diag_factor = draw_diag_factor(jax.random.fold_in(key_of[9], 71), 0)
    inverse_factor = draw_inverse_factor(jax.random.fold_in(key_of[9], 71), 0)
    diag_cotan = scatter_about(key_of[6], (NB, NB), 1.0, 6.0, ((0, 8), (1, 16)), jnp.float32)
    row_factor = scatter_about(key_of[7], (NB, K), NB ** -0.5, 0.25, ((0, 8), (1, 16)), jnp.float32)
    row_cotan = scatter_about(key_of[8], (NB, K), 1.0, 6.0, ((0, 8), (1, 16)), jnp.float32)
    return {"lower_left": lower_left, "lower_cotan": lower_cotan, "panel": panel, "panel_cotan": panel_cotan, "diag_factor": diag_factor, "inverse_factor": inverse_factor, "diag_cotan": diag_cotan, "row_factor": row_factor, "row_cotan": row_cotan}


def product(left, right):
    return jnp.dot(left.astype(jnp.float32), right.astype(jnp.float32), precision=lax.Precision.HIGHEST, preferred_element_type=jnp.float32)

def lower_half(matrix):
    return jnp.tril(matrix) - 0.5 * jnp.diag(jnp.diag(matrix))

def reference(lower_left, lower_cotan, panel, panel_cotan, diag_factor, inverse_factor, diag_cotan, row_factor, row_cotan):
    solved = product(panel_cotan, inverse_factor)
    lower_grad = lower_cotan - product(solved, row_factor)
    diag_step = diag_cotan - jnp.tril(product(solved.T, panel))
    inner = lower_half(product(diag_factor.T, diag_step))
    diag_grad = lower_half(product(product(inverse_factor.T, inner), inverse_factor))
    both = diag_grad + diag_grad.T
    row_grad = row_cotan - product(solved.T, lower_left) - product(both, row_factor)
    return (lower_grad, solved, diag_grad, row_grad)
```

```python
import jax
import jax.numpy as jnp
from jax import lax
from jax.sharding import PartitionSpec as P


X_HI, Y, Z, X_LO, CORE = 2, 4, 4, 2, 2
ROWS, COLS = X_HI * Y, Z * X_LO * CORE
BOTH = ("row", "col")


def shift(value, x_hi=0, y=0, z=0, x_lo=0, core=0):
    pairs = []
    for r in range(ROWS):
        for c in range(COLS):
            r2 = (r // Y + x_hi) % X_HI * Y + (r % Y + y) % Y
            c2 = (c // 4 + z) % Z * 4 + (c // 2 + x_lo) % X_LO * 2 + (c + core) % CORE
            pairs.append((r * COLS + c, r2 * COLS + c2))
    return lax.ppermute(value, BOTH, pairs)


def dot(a, b, ca, cb, precision=lax.Precision.HIGH):
    return lax.dot_general(
        a, b, (((ca,), (cb,)), ((), ())), precision=precision, preferred_element_type=jnp.float32
    )


def exact(a, b, ca, cb):
    return dot(a, b, ca, cb, lax.Precision.HIGHEST)


def in_order(mine, other, position, axis):
    first = position == 0
    return jnp.stack([jnp.where(first, mine, other), jnp.where(first, other, mine)], axis)


def gather4(mine, position, axis):
    behind = shift(mine, **{axis: 1})
    across = shift(mine, **{axis: 2})
    ahead = shift(mine, **{axis: -1})
    parts = (mine, behind, across, ahead)
    out = jnp.zeros((4,) + mine.shape, mine.dtype)
    for back, part in zip((0, 1, 2, 3), parts):
        out = lax.dynamic_update_slice_in_dim(out, part[None], (position - back) % 4, 0)
    return out


def everyone(value, axis, size):
    return lax.all_to_all(jnp.broadcast_to(value[None], (size,) + value.shape), axis, 0, 0, tiled=True)


def local(
    lower_left,
    lower_cotan,
    panel,
    panel_cotan,
    diag_factor,
    inverse_factor,
    diag_cotan,
    row_factor,
    row_cotan,
):
    row_pos = lax.axis_index("row")
    col_pos = lax.axis_index("col")
    x_hi, y = row_pos // Y, row_pos % Y
    z, x_lo, core = col_pos // 4, col_pos // 2 % 2, col_pos % 2
    nb_row, nb_col = diag_factor.shape
    width = nb_row * ROWS
    rows = panel.shape[0]

    small = jnp.concatenate(
        [inverse_factor.T, diag_factor.T, diag_cotan.T, jnp.zeros((nb_col, nb_row), jnp.float32)], 1
    )
    mine = panel_cotan.T
    other = shift(mine, x_lo=1)
    slices = everyone(small, "row", ROWS)

    def column(i):
        return slices[:, :, i * nb_row : (i + 1) * nb_row].transpose(1, 0, 2).reshape(nb_col, width)

    inv_t_mine, factor_t_mine, cotan_t = column(0), column(1), column(2)
    pair = in_order(mine, other, x_lo, 0).reshape(2 * nb_col, rows)
    extra = jnp.concatenate([inv_t_mine, factor_t_mine], 0)
    quads = gather4(jnp.concatenate([pair, extra], 1), z, "z")
    a_half = quads[:, :, :rows]
    e_quad = quads[:, :, rows:]
    a_other = shift(a_half, core=1)
    e_half = in_order(e_quad, shift(e_quad, x_lo=1), x_lo, 1)
    a_t = in_order(
        a_half.reshape(Z, X_LO, nb_col, rows), a_other.reshape(Z, X_LO, nb_col, rows), core, 2
    ).reshape(width, rows)
    e_full = in_order(e_half, shift(e_half, core=1), core, 2)
    inv_t = e_full[:, :, :, :nb_col].reshape(width, width)
    factor_t = e_full[:, :, :, nb_col:].reshape(width, width)

    r_half = gather4(row_factor, y, "y")
    r_full = in_order(r_half, shift(r_half, x_hi=1), x_hi, 0).reshape(width, row_factor.shape[1])

    s_part = dot(panel, a_t, 0, 1)
    s_t = everyone(s_part, "row", ROWS).sum(0)
    cross = dot(a_t, lower_left, 1, 0)
    turned = dot(inv_t, cross, 1, 0)

    blocks = turned.reshape(X_HI, Y, nb_row, -1)

    def block(i):
        return lax.dynamic_index_in_dim(blocks, (y + i) % Y, 1, keepdims=False)

    total = block(0) + shift(block(1), y=1) + shift(block(2), y=2) + shift(block(3), y=-1)
    keep = lax.dynamic_index_in_dim(total, x_hi, 0, keepdims=False)
    give = lax.dynamic_index_in_dim(total, 1 - x_hi, 0, keepdims=False)
    cross_part = keep + shift(give, x_hi=1)

    at_col = lax.broadcasted_iota(jnp.int32, (nb_col, width), 0) + col_pos * nb_col
    at_row = lax.broadcasted_iota(jnp.int32, (nb_col, width), 1)
    lower = at_row >= at_col
    step_t = cotan_t - jnp.where(lower, exact(s_t, inv_t, 1, 1), 0.0)
    inner_t = exact(step_t, factor_t, 1, 1)
    inner_t = jnp.where(lower, jnp.where(at_row == at_col, 0.5 * inner_t, inner_t), 0.0)
    x_t = exact(inner_t, inv_t, 1, 1)
    x_t = everyone(x_t, "col", COLS).reshape(width, width)

    inv_t_rows = lax.dynamic_slice_in_dim(inv_t, row_pos * nb_row, nb_row, 0)
    full = exact(x_t, inv_t, 0, 1)
    low = lax.dynamic_slice_in_dim(full, row_pos * nb_row, nb_row, 0)
    high = exact(inv_t_rows, x_t, 1, 0)
    i = lax.broadcasted_iota(jnp.int32, (nb_row, width), 0) + row_pos * nb_row
    j = lax.broadcasted_iota(jnp.int32, (nb_row, width), 1)
    both = jnp.where(i >= j, low, high)
    own = lax.dynamic_slice_in_dim(exact(x_t, inv_t_mine, 0, 1), row_pos * nb_row, nb_row, 0)
    i = lax.broadcasted_iota(jnp.int32, (nb_row, nb_col), 0) + row_pos * nb_row
    j = lax.broadcasted_iota(jnp.int32, (nb_row, nb_col), 1) + col_pos * nb_col
    diag_grad = jnp.where(i > j, own, jnp.where(i == j, 0.5 * own, 0.0))

    panel_grad = dot(a_t, inv_t_mine, 0, 1)
    spread = dot(inv_t, r_full, 0, 0)
    lower_grad = lower_cotan - dot(a_t, spread, 0, 0)
    row_grad = row_cotan - cross_part - dot(both, r_full, 1, 0)
    return (lower_grad, panel_grad, diag_grad, row_grad)


def solution(mesh):
    placed = (P("row", "col"),) * 9
    return jax.shard_map(
        local, mesh=mesh, in_specs=placed, out_specs=(P("row", "col"),) * 4, check_vma=False
    )
```

```python
import jax
import jax.numpy as jnp
from jax import lax
from jax.experimental import pallas as pl
from jax.experimental.pallas import tpu as pltpu
from jax.sharding import PartitionSpec as P


X_HI, Y, Z, X_LO, CORE = 2, 4, 4, 2, 2
ROWS, COLS = X_HI * Y, Z * X_LO * CORE
BOTH = ("row", "col")
F32, BF16 = jnp.float32, jnp.bfloat16
AT_ROW, MY_ROW, MY_COL = 16, 24, 25


def shift(value, x_hi=0, y=0, z=0, x_lo=0, core=0):
    pairs = []
    for r in range(ROWS):
        for c in range(COLS):
            r2 = (r // Y + x_hi) % X_HI * Y + (r % Y + y) % Y
            c2 = (c // 4 + z) % Z * 4 + (c // 2 + x_lo) % X_LO * 2 + (c + core) % CORE
            pairs.append((r * COLS + c, r2 * COLS + c2))
    return lax.ppermute(value, BOTH, pairs)


def ring4(value, axis):
    return [value] + [shift(value, **{axis: -s if s < 3 else 1}) for s in (1, 2, 3)]


def after(value, *others):
    return lax.optimization_barrier((value,) + others)[0]


def split(value):
    high = value.astype(BF16)
    return high, (value - high.astype(F32)).astype(BF16)


def dot(a, b, ca=1, cb=0):
    return lax.dot_general(a, b, (((ca,), (cb,)), ((), ())), preferred_element_type=F32)


def dot_high(a, b, ca, cb):
    return lax.dot_general(
        a, b, (((ca,), (cb,)), ((), ())), precision=lax.Precision.HIGH, preferred_element_type=F32
    )


def dot3(a, b, ca=1, cb=0):
    return dot(a[0], b[0], ca, cb) + (dot(a[0], b[1], ca, cb) + dot(a[1], b[0], ca, cb))


def call(body, table, args, out_shapes, flops, scratch=(), far=0, limit=16):
    vmem, hbm = pl.BlockSpec(memory_space=pltpu.VMEM), pl.BlockSpec(memory_space=pltpu.HBM)
    size = sum(a.size * a.dtype.itemsize for a in list(args) + list(out_shapes))
    return pl.pallas_call(
        body,
        out_shape=out_shapes,
        in_specs=[pl.BlockSpec(memory_space=pltpu.SMEM)] + [hbm] * far + [vmem] * (len(args) - far),
        out_specs=[vmem] * len(out_shapes),
        scratch_shapes=list(scratch),
        compiler_params=pltpu.CompilerParams(vmem_limit_bytes=limit << 20),
        cost_estimate=pl.CostEstimate(flops=int(flops), bytes_accessed=int(size), transcendentals=0),
    )(table, *args)


def fetch(pairs, sems):
    copies = [pltpu.make_async_copy(src, dst, sems.at[n]) for n, (src, dst) in enumerate(pairs)]
    for copy in copies:
        copy.start()
    for copy in copies:
        copy.wait()


def out(shape, dtype=F32):
    return jax.ShapeDtypeStruct(shape, dtype)


def unpack_body(tab, *refs):
    extra, cotan, tall = refs[8:]
    for n, piece in enumerate(refs[:8]):
        tall[pl.ds(pl.multiple_of(tab[AT_ROW + n] * 64, 64), 64), :] = piece[...]
    flat = tall[...].T
    extra[...] = flat[0:64, :]
    cotan[...] = flat[64:96, :]


def chain_body(tab, e0, e1, e2, e3, sums, cotan, inv_t, stepped, res, fac_t):
    for f, s, d in ((f, s, d) for f in range(2) for s in range(4) for d in range(2)):
        piece = ((e0, e1), (e2, e3))[f][d]
        at = pl.ds(pl.multiple_of(tab[f * 8 + s * 2 + d] * 32, 32), 32)
        inv_t[at, :] = piece[s, 0:32, :]
        fac_t[at, :] = piece[s, 32:64, :]
    for n in range(8):
        at = pl.ds(pl.multiple_of(tab[AT_ROW + n] * 64, 64), 64)
        stepped[n * 64 : n * 64 + 64, :] = inv_t[at, :]
    total = sums[0]
    for r in range(1, ROWS):
        total = total + sums[r]
    inverse = split(inv_t[...].T)
    j = lax.broadcasted_iota(jnp.int32, (32, 512), 1)
    c = lax.broadcasted_iota(jnp.int32, (32, 512), 0) + tab[MY_COL] * 32
    step = cotan[...] - jnp.where(j >= c, dot3(split(total), inverse), 0.0)
    inner = dot3(split(step), split(fac_t[...].T))
    inner = jnp.where(j > c, inner, jnp.where(j == c, 0.5 * inner, 0.0))
    x = dot3(split(inner), inverse)
    for r in range(COLS):
        res[r] = x


def near_body(tab, *refs):
    res = refs[8]
    for n, piece in enumerate(refs[:8]):
        res[pl.ds(pl.multiple_of((tab[n] >> 1) * 32, 32), 32), :] = piece[...]


def panel_body(tab, near, far, res):
    core = tab[MY_COL] & 1
    for n in range(8):
        at = n * 32
        res[pl.ds(pl.multiple_of((n * 2 + core) * 32, 32), 32), :] = near[at : at + 32, :]
        res[pl.ds(pl.multiple_of((n * 2 + 1 - core) * 32, 32), 32), :] = far[at : at + 32, :]


def rows_body(tab, *refs):
    res, sems = refs[8:]
    pairs = []
    for n, piece in enumerate(refs[:8]):
        at = pl.ds(pl.multiple_of(tab[AT_ROW + n] * 64, 64), 64)
        pairs.append((piece, res.at[at]))
    fetch(pairs, sems)


def tail_body(tab, kept_far, come_far, cotan_far, rows_far, inv_far, xs, mine, row, diag, kept, come, cotan, rows, inv_t, sems):
    fars, nears = (inv_far, rows_far, kept_far, come_far, cotan_far), (inv_t, rows, kept, come, cotan)
    copies = [pltpu.make_async_copy(src, dst, sems.at[n]) for n, (src, dst) in enumerate(zip(fars, nears))]
    for copy in copies:
        copy.start()
    x = split(xs[...])
    copies[0].wait()
    high = dot3(split(inv_t[pl.ds(pl.multiple_of(tab[MY_ROW] * 64, 64), 64), :]), x)
    i = lax.broadcasted_iota(jnp.int32, (512, 64), 0)
    j = lax.broadcasted_iota(jnp.int32, (512, 64), 1) + tab[MY_ROW] * 64
    pick = jnp.where(i == j, 1.0, 0.0).astype(BF16)
    x_rows = (dot(x[0], pick).astype(BF16), dot(x[1], pick).astype(BF16))
    low_t = dot3(split(inv_t[...]), x_rows)
    corner_t = dot3(split(mine[...]), x_rows)
    i = lax.broadcasted_iota(jnp.int32, (64, 512), 0) + tab[MY_ROW] * 64
    j = lax.broadcasted_iota(jnp.int32, (64, 512), 1)
    both = split(jnp.where(i >= j, low_t.T, high))
    for copy in copies[1:]:
        copy.wait()
    row[...] = cotan[...] - (kept[...] + come[...]) - dot3(both, split(rows[...]))
    i = lax.broadcasted_iota(jnp.int32, (32, 64), 1) + tab[MY_ROW] * 64
    j = lax.broadcasted_iota(jnp.int32, (32, 64), 0) + tab[MY_COL] * 32
    diag[...] = jnp.where(i > j, corner_t, jnp.where(i == j, 0.5 * corner_t, 0.0)).T


def local(
    lower_left,
    lower_cotan,
    panel,
    panel_cotan,
    diag_factor,
    inverse_factor,
    diag_cotan,
    row_factor,
    row_cotan,
):
    row_pos = lax.axis_index("row")
    col_pos = lax.axis_index("col")
    x_hi, y = row_pos >> 2, row_pos & 3
    z, x_lo, core = col_pos >> 2, (col_pos >> 1) & 1, col_pos & 1
    q = lax.iota(jnp.int32, 32)
    table = (((z + (q >> 1)) & 3) << 2) + ((x_lo ^ (q & 1)) << 1) + (core ^ (q >> 3))
    table = jnp.where(q >= AT_ROW, ((x_hi ^ (q & 1)) << 2) + ((y + ((q - AT_ROW) >> 1)) & 3), table)
    table = jnp.where(q == MY_ROW, row_pos, jnp.where(q == MY_COL, col_pos, table))

    mine = panel_cotan.T
    other = shift(mine, x_lo=1)
    mine3, mine1 = shift(mine, z=1), shift(mine, z=-1)
    other3, other1 = shift(other, z=1), shift(other, z=-1)
    mine2 = shift(mine3, z=1)
    other2 = shift(other1, z=-1)
    near = [mine, other, mine1, other1, mine2, other2, mine3, other3]
    half = call(near_body, table, near, (out((256, 1536)),), 1e5)[0]
    far = shift(half, core=1)
    a_t = call(panel_body, table, (half, far), (out((512, 1536)),), 1e5)[0]

    def over_row(mine):
        other = shift(mine, x_hi=1)
        mine3, mine1 = shift(mine, y=1), shift(mine, y=-1)
        other3, other1 = shift(other, y=1), shift(other, y=-1)
        mine2, other2 = shift(mine3, y=1), shift(other1, y=-1)
        return mine, other, mine1, other1, mine2, other2, mine3, other3

    pad = jnp.zeros((64, 32), F32)
    s_parts = over_row(jnp.concatenate([inverse_factor, diag_factor, diag_cotan, pad], 1))
    r_parts = over_row(row_factor)

    sums = dot_high(panel, a_t, 0, 1)
    sums = jnp.broadcast_to(sums[None], (ROWS, 32, 512))
    gathered = lax.all_to_all(sums, "row", 0, 0, tiled=True)
    cross = dot_high(after(a_t, sums), lower_left, 1, 0)

    extra, cotan_t = call(
        unpack_body, table, s_parts, (out((64, 512)), out((32, 512))), 1e5, scratch=(pltpu.VMEM((512, 128), F32),)
    )
    e0 = jnp.stack(ring4(extra, "z"))
    e2 = shift(e0, core=1)
    e1 = shift(e0, x_lo=1)
    e3 = shift(e1, core=1)
    inv_t, stepped, x_mine = call(
        chain_body, table, (e0, e1, e2, e3, gathered, cotan_t),
        (out((512, 512)), out((512, 512)), out((COLS, 32, 512))), 4e8, scratch=(pltpu.VMEM((512, 512), F32),),
    )
    x_t = lax.all_to_all(x_mine, "col", 0, 0, tiled=True).reshape(512, 512)

    turned = dot_high(stepped, cross, 1, 0).reshape(Y, 2, 64, -1)
    up, down = shift(turned[2, 0], y=1), shift(turned[2, 1], y=-1)
    up = shift(jnp.stack([turned[1, 0] + up, turned[1, 1]]), y=1)
    down = shift(jnp.stack([turned[3, 0], turned[3, 1] + down]), y=-1)
    come = shift(turned[0, 1] + up[1] + down[1], x_hi=1)
    kept = turned[0, 0] + up[0] + down[0]

    r_full = call(
        rows_body, table, r_parts, (out((512, 1024)),), 1e5, scratch=(pltpu.SemaphoreType.DMA((8,)),), far=8
    )[0]

    spread = dot_high(inv_t, r_full, 0, 0)
    lower_grad = lower_cotan - dot_high(a_t, spread, 0, 0)
    panel_grad = dot_high(a_t, extra[:32], 0, 1)
    row_grad, diag_grad = call(
        tail_body, table, (kept, come, row_cotan, r_full, inv_t, x_t, extra[:32]),
        (out((64, 1024)), out((64, 32))), 4e8,
        scratch=(pltpu.VMEM((64, 1024), F32),) * 3
        + (pltpu.VMEM((512, 1024), F32), pltpu.VMEM((512, 512), F32), pltpu.SemaphoreType.DMA((5,))), far=5, limit=56,
    )
    return (lower_grad, panel_grad, diag_grad, row_grad)


def solution(mesh):
    placed = (P("row", "col"),) * 9

    return jax.shard_map(local, mesh=mesh, in_specs=placed, out_specs=(P("row", "col"),) * 4, check_vma=False)
```
